256 devices in a mesh: seq: 64 (over z, x, core), head: 4 (over y).
Axes of the slice: x: 4, y: 4, z: 8, core: 2. Of those that a mesh axis runs over, the one named last changes fastest.
Arguments:
- queries: bfloat16 [8192, 4096], P('seq', 'head'), may hold values from -6 to 6, as said below
- keys: bfloat16 [8192, 4096], P('seq', 'head'), may hold values from -6 to 6, as said below
- values: bfloat16 [8192, 4096], P('seq', 'head'), may hold values from -6 to 6
- transitions: bfloat16 [8192, 4096], P('seq', 'head'), may hold values from -6 to 6, as said below
- betas: bfloat16 [8192, 32], P('seq', 'head'), may hold values from 0.19921875 to 1.5
- segments: int32 [8192], replicated, may hold values from 0 to 15, never falling along the last dimension, each value on 1 to 1024 neighbouring positions
- visits: int32 [64, 3], P('seq'), may hold values 0 or 1
Outputs:
- attended: bfloat16 [8192, 4096], P('seq', 'head')
The draws below stay inside these ranges and needn't reach their ends.
Inputs may be any that keep to these rules, and one draw needn't show every extreme that they name: `queries`: real-valued entries. `keys`: real-valued entries. `transitions`: real-valued entries, no head row all zero.
All inputs are finite; a program needn't handle non-finite values. No bound on the sum of `visits` on one device may be relied on, other than what follows from the above.
Results may differ from the reference program's by a relative error of at most 0.0036.
Values may be sent and summed in bfloat16 or wider, within the bound.
No kernel may reach another device: no remote copies, remote signals or barrier semaphores. Data moves between devices by JAX's collectives and lax.ppermute only.
A program may use at most 64 MiB of HBM per device.

```python
import math
import jax
import jax.numpy as jnp
import numpy as np
from jax import lax

HEADS = 32
HEAD_DIM = 128
TOK_DEV = 128
BACK = 3
BLOCKS = 64
TOKENS = 8192
DOCS = 16


def base_draw(key, salt):
    noise_key = jax.random.fold_in(key, salt)
    return jnp.clip(jax.random.normal(noise_key, (TOKENS, HEADS * HEAD_DIM), jnp.float32), -4.0, 4.0)


def draw_queries(key, part):
    tensor = base_draw(key, 11)
    return tensor.astype(jnp.bfloat16)


def draw_keys(key, part):
    tensor = base_draw(key, 23)
    return tensor.astype(jnp.bfloat16)


def draw_transitions(key, part):
    tensor = base_draw(key, 37)
    return tensor.astype(jnp.bfloat16)


def touch_ends(result, own_key, low, high):
    shape = result.shape
    spot = [jax.random.randint(jax.random.fold_in(own_key, axis), (), 0, shape[axis]) for axis in range(len(shape))]
    result = result.at[tuple(spot)].set(low)
    longest = shape.index(max(shape))
    spot[longest] = (spot[longest] + 1) % shape[longest]
    return result.at[tuple(spot)].set(high)


def block_scale(key, extent, shards, smallest, largest):
    gain = 1.0
    for dim, blocks in shards:
        draws = jax.random.uniform(jax.random.fold_in(jax.random.fold_in(key, 6), dim), (blocks,), jnp.float32, smallest / len(shards), largest / len(shards))
        gain = gain * jnp.repeat(jnp.exp(draws), extent[dim] // blocks).reshape((-1,) + (1,) * (len(extent) - 1 - dim))
    return gain


def profile(amount, total, limit, lean):
    loads = [(1 << 20) // math.isqrt(grade ** lean) + 1 for grade in range(2, amount + 1)]
    rest, counts = total - limit - (amount - 1), [1] * (amount - 1)
    while rest > 0:
        movable = [i for i in range(amount - 1) if counts[i] < limit]
        whole, budget = sum([loads[i] for i in movable]), rest
        for i in movable:
            addition = min(limit - counts[i], max(1, budget * loads[i] // whole), rest)
            counts[i] = counts[i] + addition
            rest = rest - addition
    return np.array([limit] + counts)


def uneven_parts(rng, amount, total, limit, slope):
    if amount == 2:
        one = jax.random.randint(rng, (), max(1, total - limit), min(limit, total - 1) + 1)
        return jnp.stack([one, total - one])
    lengths = jnp.asarray(profile(amount, total, limit, slope), jnp.int32)
    pairs = (amount - 1) // 2
    donor, sink = lengths[1:1 + 2 * pairs:2], lengths[2:2 + 2 * pairs:2]
    room = jnp.minimum(donor - 1, limit - sink)
    passed = jax.random.randint(jax.random.fold_in(rng, 1), (pairs,), 0, 1 << 20) % (room + 1)
    lengths = lengths.at[1:1 + 2 * pairs:2].set(donor - passed).at[2:2 + 2 * pairs:2].set(sink + passed)
    return lengths[jax.random.permutation(jax.random.fold_in(rng, 2), amount)]


def scatter_about(rng, extent, scale, bound, cuts=(), kind=jnp.bfloat16):
    entries = jax.random.normal(rng, extent, jnp.float32) * scale
    if len(cuts) > 0:
        entries = block_scale(rng, extent, cuts, -0.22, 0.18) * entries
    return jnp.clip(entries, min=-bound, max=bound).astype(kind)


def setup_inputs(seed: int = 0) -> dict:
    splits = jax.random.split(jax.random.key(seed), 8)
    return {
        "queries": draw_queries(jax.random.fold_in(splits[7], 71), 0),
        "keys": draw_keys(jax.random.fold_in(splits[7], 71), 0),
        "values": scatter_about(splits[2], (TOKENS, HEADS * HEAD_DIM), 1.0, 6.0, ((0, 64), (1, 4))),
        "transitions": draw_transitions(jax.random.fold_in(splits[7], 71), 0),
        "betas": jnp.clip(jnp.exp(math.log(1.5) - 2.018817 * jax.random.uniform(splits[4], (TOKENS, HEADS), jnp.float32) ** block_scale(splits[4], (TOKENS, HEADS), ((0, 64), (1, 4)), -0.2, 0.2)), 0.19921875, 1.5).astype(jnp.bfloat16),
        "segments": jnp.searchsorted(jnp.cumsum(uneven_parts(splits[5], DOCS, TOKENS, min(8 * TOK_DEV, TOKENS // 2), 2)), jnp.arange(TOKENS), side="right").astype(jnp.int32),
        "visits": touch_ends((jax.random.randint(splits[6], (BLOCKS, BACK), 0, 4) < 3).astype(jnp.int32), jax.random.fold_in(splits[6], 1), 0, 1),
    }


HIGHEST = lax.Precision.HIGHEST
EPSILON = 1e-06

def heads_first(block, head_count):
    height = block.shape[0]
    return jnp.transpose(block.reshape(height, head_count, -1), (1, 0, 2))

def transition_parts(key_rows, raw_w, strength):
    length = key_rows.shape[1]
    width = key_rows.shape[2]
    unit_w = raw_w / jnp.sqrt(lax.optimization_barrier(jnp.sum(raw_w * raw_w, axis=-1, keepdims=True)) + EPSILON)
    strict = jnp.tril(jnp.ones((length, length), jnp.float32), -1)
    gram_mat = jnp.einsum('htd,hsd->hts', unit_w, unit_w, precision=HIGHEST)
    lower_mat = jnp.eye(length, dtype=jnp.float32)[None] + strict[None] * strength[:, :, None] * gram_mat
    cross_terms = jnp.einsum('htd,hjd->htj', unit_w, key_rows, precision=HIGHEST)
    right_side = jnp.concatenate([strength[:, :, None] * unit_w, strict[None] * strength[:, :, None] * cross_terms], axis=-1)
    solved = lax.linalg.triangular_solve(lower_mat, right_side, left_side=True, lower=True, unit_diagonal=True)
    back_rows = solved[:, :, :width]
    carry_coef = solved[:, :, width:]
    carried = key_rows - jnp.einsum('htj,htd->hjd', carry_coef, unit_w, precision=HIGHEST)
    return (unit_w, back_rows, carry_coef, carried)

def query_parts(query_rows, key_rows, unit_w, back_rows, carry_coef):
    length = query_rows.shape[1]
    inclusive = jnp.tril(jnp.ones((length, length), jnp.float32))
    query_w = jnp.einsum('hid,htd->hit', query_rows, unit_w, precision=HIGHEST) * inclusive[None]
    turned = query_rows - jnp.einsum('hit,htd->hid', query_w, back_rows, precision=HIGHEST)
    own_scores = jnp.einsum('hid,hjd->hij', query_rows, key_rows, precision=HIGHEST)
    own_scores = own_scores - jnp.einsum('hit,htj->hij', query_w, carry_coef, precision=HIGHEST)
    return (turned, own_scores)

def advance(carried, back_rows, unit_w):
    inner = jnp.einsum('hjd,htd->hjt', carried, back_rows, precision=HIGHEST)
    return carried - jnp.einsum('hjt,htd->hjd', inner, unit_w, precision=HIGHEST)

def weights_of(turned, own_scores, far_keys, seg_keys, seg_query, visit_row):
    length = own_scores.shape[1]
    cross_terms = jnp.einsum('hid,hjd->hij', turned, far_keys, precision=HIGHEST)
    scores = jnp.concatenate([cross_terms, own_scores], axis=-1) * HEAD_DIM ** (-0.5)
    spread = scores.shape[2]
    visited = jnp.concatenate([visit_row[::-1], jnp.ones((1,), jnp.int32)])
    visited = jnp.repeat(visited, length, total_repeat_length=spread)
    column = jnp.arange(spread, dtype=jnp.int32)
    row_ids = jnp.arange(length, dtype=jnp.int32)
    allowed = (visited[None, :] > 0) & (seg_keys[None, :] == seg_query[:, None])
    allowed = allowed & (column[None, :] <= row_ids[:, None] + (spread - length))
    scores = jnp.where(allowed[None], scores, -1e+30)
    row_max = lax.optimization_barrier(jnp.max(scores, axis=-1, keepdims=True))
    weights = jnp.exp(scores - row_max)
    total_w = lax.optimization_barrier(jnp.sum(weights, axis=-1, keepdims=True))
    return (weights.astype(jnp.bfloat16), total_w)

def reference(queries, keys, values, transitions, betas, segments, visits):
    length = TOK_DEV

    def by_block(tensor):
        return tensor.reshape(BLOCKS, length, tensor.shape[1])
    query_blocks = by_block(queries)
    key_blocks = by_block(keys)
    value_blocks = by_block(values)
    trans_blocks = by_block(transitions)
    beta_blocks = by_block(betas)

    def prepare(pieces):
        key_part, trans_part, beta_part = pieces
        unit_w, back_rows, carry_coef, carried = transition_parts(heads_first(key_part.astype(jnp.float32), HEADS), heads_first(trans_part.astype(jnp.float32), HEADS), beta_part.astype(jnp.float32).T)
        return (unit_w, back_rows, carried)
    units, backs, carried_all = lax.map(prepare, (key_blocks, trans_blocks, beta_blocks))
    moving = carried_all
    carried_list = []
    for distance in range(BACK):
        moving = jnp.concatenate([jnp.zeros_like(moving[:1]), moving[:-1]], axis=0)
        carried_list.append(moving)
        if distance + 1 < BACK:
            moving = jax.vmap(advance)(moving, backs, units)
    near_keys = jnp.concatenate(carried_list[::-1], axis=2)
    value_pad = jnp.concatenate([jnp.zeros((BACK * length, values.shape[1]), jnp.bfloat16), values], axis=0)
    segment_pad = jnp.concatenate([jnp.full((BACK * length,), -1, jnp.int32), segments.astype(jnp.int32)])

    def finish(pieces):
        block_index, query_part, key_part, trans_part, beta_part, far_keys = pieces
        key_rows = heads_first(key_part.astype(jnp.float32), HEADS)
        unit_w, back_rows, carry_coef, carried = transition_parts(key_rows, heads_first(trans_part.astype(jnp.float32), HEADS), beta_part.astype(jnp.float32).T)
        turned, own_scores = query_parts(heads_first(query_part.astype(jnp.float32), HEADS), key_rows, unit_w, back_rows, carry_coef)
        start = (block_index * length).astype(jnp.int32)
        seg_keys = lax.dynamic_slice_in_dim(segment_pad, start, (BACK + 1) * length)
        value_rows = lax.dynamic_slice_in_dim(value_pad, start, (BACK + 1) * length)
        visit_row = lax.dynamic_index_in_dim(visits, block_index, 0, keepdims=False).astype(jnp.int32)
        weights, total_w = weights_of(turned, own_scores, far_keys, seg_keys, seg_keys[BACK * length:], visit_row)
        mixed = jnp.einsum('hij,hjd->hid', weights.astype(jnp.float32), heads_first(value_rows, HEADS).astype(jnp.float32), precision=HIGHEST) / total_w
        return jnp.transpose(mixed, (1, 0, 2)).reshape(length, -1).astype(jnp.bfloat16)
    results = lax.map(finish, (jnp.arange(BLOCKS, dtype=jnp.int32), query_blocks, key_blocks, trans_blocks, beta_blocks, near_keys))
    return results.reshape(TOKENS, -1)
```

```python
import jax
import jax.numpy as jnp
from jax import lax
from jax.experimental import pallas as pl
from jax.experimental.pallas import tpu as pltpu
from jax.sharding import PartitionSpec as P

HEAD_DIM = 128
BACK = 3
EPSILON = 1e-06
F32 = jnp.float32
BF16 = jnp.bfloat16
VMEM_LIMIT = 48 << 20


def dot_nn(left, right):
    return lax.dot_general(left, right, (((1,), (0,)), ((), ())), preferred_element_type=F32)


def dot_nt(left, right):
    return lax.dot_general(left, right, (((1,), (1,)), ((), ())), preferred_element_type=F32)


def columns(head):
    return slice(head * HEAD_DIM, (head + 1) * HEAD_DIM)


def upper_inverse(strict_uppers, row, col):
    size = row.shape[0]
    eye = jnp.where(row == col, 1.0, 0.0).astype(F32)
    base = 16
    same = (row // base) == (col // base)
    diag = [jnp.where(same, u, 0.0) for u in strict_uppers]
    power = [d.astype(BF16) for d in diag]
    inverse = [eye - d for d in diag]
    reach = 2
    while reach < base:
        power = [dot_nn(p, p).astype(BF16) for p in power]
        inverse = [x + dot_nn(x.astype(BF16), p) for x, p in zip(inverse, power)]
        reach *= 2
    span = 2 * base
    while span <= size:
        joined = ((row // span) == (col // span)) & ((row // (span // 2)) != (col // (span // 2)))
        corner = [jnp.where(joined, u, 0.0).astype(BF16) for u in strict_uppers]
        half = [x.astype(BF16) for x in inverse]
        mid = [dot_nn(x, e).astype(BF16) for x, e in zip(half, corner)]
        inverse = [x - dot_nn(m, y) for x, m, y in zip(inverse, mid, half)]
        span *= 2
    return inverse


def prep_kernel(k_ref, w_ref, beta_ref, wb_ref, bt_ref, cct_ref, c_ref, d_ref):
    heads = beta_ref.shape[1]
    length = k_ref.shape[0]
    row = lax.broadcasted_iota(jnp.int32, (length, length), 0)
    col = lax.broadcasted_iota(jnp.int32, (length, length), 1)
    upper = row < col
    units, turned_units, uppers, rights = [], [], [], []
    for h in range(heads):
        w = w_ref[:, columns(h)].astype(F32)
        scale = lax.rsqrt(jnp.sum(w * w, axis=-1, keepdims=True) + EPSILON)
        unit = w * scale
        wb = unit.astype(BF16)
        bw = unit * beta_ref[:, h : h + 1].astype(F32)
        units.append(wb)
        turned_units.append(jnp.transpose(bw).astype(BF16))
        wb_ref[:, columns(h)] = wb
        both = dot_nt(jnp.concatenate([wb, k_ref[:, columns(h)]], axis=0), bw.astype(BF16))
        uppers.append(jnp.where(upper, both[:length], 0.0))
        rights.append(jnp.where(upper, both[length:], 0.0).astype(BF16))
    inverse = upper_inverse(uppers, row, col)
    for h in range(heads):
        solved = dot_nn(
            jnp.concatenate([turned_units[h], rights[h]], axis=0), inverse[h].astype(BF16)
        ).astype(BF16)
        bt_ref[:, columns(h)] = solved[:length]
        cct_ref[:, columns(h)] = solved[length:]
        moved = dot_nn(solved, units[h])
        d_ref[:, columns(h)] = moved[:length].astype(BF16)
        c_ref[:, columns(h)] = (k_ref[:, columns(h)].astype(F32) - moved[length:]).astype(BF16)


def query_kernel(q_ref, k_ref, wb_ref, bt_ref, cct_ref, t_ref, own_ref):
    length = q_ref.shape[0]
    row = lax.broadcasted_iota(jnp.int32, (length, length), 0)
    col = lax.broadcasted_iota(jnp.int32, (length, length), 1)
    for h in range(q_ref.shape[1] // HEAD_DIM):
        q = q_ref[:, columns(h)]
        both = dot_nt(q, jnp.concatenate([wb_ref[:, columns(h)], k_ref[:, columns(h)]], axis=0))
        query_w = jnp.where(col <= row, both[:, :length], 0.0).astype(BF16)
        turn = dot_nt(
            query_w, jnp.concatenate([bt_ref[:, columns(h)], cct_ref[:, columns(h)]], axis=0)
        )
        t_ref[:, columns(h)] = (q.astype(F32) - turn[:, :length]).astype(BF16)
        own_ref[:, columns(h)] = both[:, length:] - turn[:, length:]


def pair_kernel(c_ref, d_ref, other_ref, x2_ref, e_ref):
    length = c_ref.shape[0]
    for h in range(c_ref.shape[1] // HEAD_DIM):
        c, d, o = c_ref[:, columns(h)], d_ref[:, columns(h)], other_ref[:, columns(h)]
        both = dot_nn(jnp.concatenate([c, d], axis=0), o)
        x2_ref[:, columns(h)] = (c.astype(F32) - both[:length]).astype(BF16)
        e_ref[:, columns(h)] = (d.astype(F32) + o.astype(F32) - both[length:]).astype(BF16)


def third_kernel(x1_ref, e_ref, x3_ref):
    for h in range(x1_ref.shape[1] // HEAD_DIM):
        x = x1_ref[:, columns(h)]
        x3_ref[:, columns(h)] = (x.astype(F32) - dot_nn(x, e_ref[:, columns(h)])).astype(BF16)


def final_kernel(
    visits_ref, seg_ref, t_ref, other_ref, own_ref, v_ref, near_k_ref, near_v_ref,
    even_k2, even_v2, even_k3, even_v3, odd_k2, odd_v2, odd_k3, odd_v3,
    out_ref, k2, v2, k3, v3, t2, sems,
):
    length = t_ref.shape[0]
    block = lax.axis_index("seq")
    odd = lax.rem(block, 2)
    targets = (k2, v2, k3, v3)

    @pl.when(odd == 0)
    def _():
        for i, (src, dst) in enumerate(zip((even_k2, even_v2, even_k3, even_v3), targets)):
            pltpu.make_async_copy(src, dst, sems.at[i]).start()
        t2[...] = t_ref[...]

    @pl.when(odd == 1)
    def _():
        for i, (src, dst) in enumerate(zip((odd_k2, odd_v2, odd_k3, odd_v3), targets)):
            pltpu.make_async_copy(src, dst, sems.at[i]).start()
        for h in range(t_ref.shape[1] // HEAD_DIM):
            t = t_ref[:, columns(h)]
            t2[:, columns(h)] = (t.astype(F32) - dot_nt(t, other_ref[:, columns(h)])).astype(BF16)

    row = lax.broadcasted_iota(jnp.int32, (length, length), 0)
    col = lax.broadcasted_iota(jnp.int32, (length, length), 1)

    def seg_row(r):
        at = jnp.maximum(block - r, 0)
        return seg_ref[pl.ds(at, 1), :].astype(F32)

    seg_q = jnp.transpose(jnp.broadcast_to(seg_row(0), (length, length)))
    allowed = []
    for r in (3, 2, 1):
        open_ = jnp.where(block - r >= 0, visits_ref[0, r - 1], 0)
        allowed.append((seg_q == seg_row(r)) & (open_ > 0))
    allowed.append((seg_q == seg_row(0)) & (col <= row))
    allow = jnp.concatenate([jnp.where(a, 0.0, -1e30) for a in allowed], axis=1)
    for i, dst in enumerate(targets):
        pltpu.make_async_copy(dst, dst, sems.at[i]).wait()
    for h in range(t_ref.shape[1] // HEAD_DIM):
        c = columns(h)
        far = dot_nt(t2[:, c], jnp.concatenate([k3[:, c], k2[:, c]], axis=0))
        near = dot_nt(t_ref[:, c], near_k_ref[:, c])
        scores = jnp.concatenate([far, near, own_ref[:, c]], axis=1) * HEAD_DIM**-0.5 + allow
        top = jnp.max(scores, axis=-1, keepdims=True)
        weights = jnp.exp(scores - top)
        total = jnp.sum(weights, axis=-1, keepdims=True)
        rows = jnp.concatenate([v3[:, c], v2[:, c], near_v_ref[:, c], v_ref[:, c]], axis=0)
        out_ref[:, c] = (dot_nn(weights.astype(BF16), rows) / total).astype(BF16)


def call(body, outs, *args, scratch=(), specs=None, flops=0, name=None):
    size = sum(a.size * a.dtype.itemsize for a in args) + sum(o.size * o.dtype.itemsize for o in outs)
    vmem = pl.BlockSpec(memory_space=pltpu.VMEM)
    return pl.pallas_call(
        body,
        out_shape=outs,
        in_specs=specs or [vmem] * len(args),
        out_specs=[vmem] * len(outs),
        scratch_shapes=scratch,
        compiler_params=pltpu.CompilerParams(vmem_limit_bytes=VMEM_LIMIT),
        cost_estimate=pl.CostEstimate(flops=flops, bytes_accessed=size, transcendentals=0),
        name=name,
    )(*args)


def shards(queries, keys, values, transitions, betas, segments, visits):
    shape = jax.ShapeDtypeStruct(queries.shape, BF16)
    wide = jax.ShapeDtypeStruct(queries.shape, F32)
    size = lax.axis_size("seq")
    next_one = [(i, i + 1) for i in range(size - 1)]
    swap = [(i, i ^ 1) for i in range(size)]
    next_even = [(i, i + 2) for i in range(0, size - 2, 2)]
    to_odd = [(i, i + 1) for i in range(0, size, 2)]

    near_v = lax.ppermute(values, "seq", next_one)
    unit, back_t, coef_t, carried, op = call(
        prep_kernel, [shape] * 5, keys, transitions, betas, name="prep"
    )
    near_k = lax.ppermute(carried, "seq", next_one)
    other = lax.ppermute(op, "seq", swap)
    turned, own = call(
        query_kernel, [shape, wide], queries, keys, unit, back_t, coef_t, name="query"
    )
    far2, both = call(pair_kernel, [shape] * 2, carried, op, other, name="pair")
    even_v2 = lax.ppermute(values, "seq", next_even)
    even_k2 = lax.ppermute(far2, "seq", next_even)
    (far3,) = call(third_kernel, [shape], near_k, both, name="third")
    even_k3 = lax.ppermute(far3, "seq", next_even)
    even_v3 = lax.ppermute(near_v, "seq", next_even)
    odd_k2 = lax.ppermute(near_k, "seq", to_odd)
    odd_v2 = lax.ppermute(near_v, "seq", to_odd)
    odd_k3 = lax.ppermute(even_k2, "seq", to_odd)
    odd_v3 = lax.ppermute(even_v2, "seq", to_odd)
    vmem = pl.BlockSpec(memory_space=pltpu.VMEM)
    smem = pl.BlockSpec(memory_space=pltpu.SMEM)
    hbm = pl.BlockSpec(memory_space=pl.ANY)
    (out,) = call(
        final_kernel,
        [shape],
        visits,
        segments.reshape(size, -1),
        turned,
        other,
        own,
        values,
        near_k,
        near_v,
        even_k2,
        even_v2,
        even_k3,
        even_v3,
        odd_k2,
        odd_v2,
        odd_k3,
        odd_v3,
        specs=[smem] + [vmem] * 7 + [hbm] * 8,
        scratch=[pltpu.VMEM(queries.shape, BF16)] * 5 + [pltpu.SemaphoreType.DMA((4,))],
        name="final",
    )
    return out


def solution(mesh):
    return jax.shard_map(
        shards,
        mesh=mesh,
        in_specs=(
            P("seq", "head"),
            P("seq", "head"),
            P("seq", "head"),
            P("seq", "head"),
            P("seq", "head"),
            P(),
            P("seq", None),
        ),
        out_specs=P("seq", "head"),
        check_vma=False,
    )
```

```python
import math

import jax
import jax.numpy as jnp
from jax import lax
from jax.experimental import pallas as pl
from jax.experimental.pallas import tpu as pltpu
from jax.sharding import PartitionSpec as P

HEAD_DIM = 128
BACK = 3
EPSILON = 1e-06
GROUP = 4
F32 = jnp.float32
BF16 = jnp.bfloat16
SCALE = HEAD_DIM**-0.5 * math.log2(math.e)


def dot_nn(left, right):
    return lax.dot_general(left, right, (((1,), (0,)), ((), ())), preferred_element_type=F32)


def dot_nt(left, right):
    return lax.dot_general(left, right, (((1,), (1,)), ((), ())), preferred_element_type=F32)


def columns(head):
    return slice(head * HEAD_DIM, (head + 1) * HEAD_DIM)


def upper_inverse(strict_uppers, row, col):
    size = row.shape[0]
    eye = jnp.where(row == col, 1.0, 0.0).astype(F32)
    base = 16
    same = (row // base) == (col // base)
    diag = [jnp.where(same, u, 0.0) for u in strict_uppers]
    power = [d.astype(BF16) for d in diag]
    inverse = [eye - d for d in diag]
    reach = 2
    while reach < base:
        power = [dot_nn(p, p).astype(BF16) for p in power]
        inverse = [x + dot_nn(x.astype(BF16), p) for x, p in zip(inverse, power)]
        reach *= 2
    span = 2 * base
    while span <= size:
        joined = ((row // span) == (col // span)) & ((row // (span // 2)) != (col // (span // 2)))
        corner = [jnp.where(joined, u, 0.0).astype(BF16) for u in strict_uppers]
        half = [x.astype(BF16) for x in inverse]
        mid = [dot_nn(x, e).astype(BF16) for x, e in zip(half, corner)]
        inverse = [x - dot_nn(m, y) for x, m, y in zip(inverse, mid, half)]
        span *= 2
    return inverse


def prep_kernel(
    k_hbm, w_hbm, beta_hbm, q_hbm, wb_ref, bt_ref, cct_ref, c_ref, d_ref, k_ref, q_ref,
    w_ref, beta_ref, sems,
):
    length, width = k_ref.shape
    copies = [
        pltpu.make_async_copy(w_hbm, w_ref, sems.at[0]),
        pltpu.make_async_copy(beta_hbm, beta_ref, sems.at[2]),
        pltpu.make_async_copy(k_hbm, k_ref, sems.at[1]),
        pltpu.make_async_copy(q_hbm, q_ref, sems.at[3]),
    ]
    for copy in copies:
        copy.start()
    heads = width // HEAD_DIM
    row = lax.broadcasted_iota(jnp.int32, (length, length), 0)
    col = lax.broadcasted_iota(jnp.int32, (length, length), 1)
    upper = row < col
    copies[0].wait()
    copies[1].wait()
    beta = beta_ref[...].astype(F32)
    beta = jnp.transpose(jnp.concatenate([beta] * (length // heads), axis=0))
    units, turned_units, uppers, rights = [], [], [], []
    scaled = []
    for h in range(heads):
        w = w_ref[:, columns(h)].astype(F32)
        scale = lax.rsqrt(jnp.sum(w * w, axis=-1, keepdims=True) + EPSILON)
        unit = w * scale
        wb = unit.astype(BF16)
        bw = unit * beta[:, h : h + 1]
        units.append(wb)
        scaled.append(bw.astype(BF16))
        turned_units.append(jnp.transpose(bw).astype(BF16))
        wb_ref[:, columns(h)] = wb
    copies[2].wait()
    for h in range(heads):
        both = dot_nt(jnp.concatenate([units[h], k_ref[:, columns(h)]], axis=0), scaled[h])
        uppers.append(jnp.where(upper, both[:length], 0.0))
        rights.append(jnp.where(upper, both[length:], 0.0).astype(BF16))
    inverse = upper_inverse(uppers, row, col)
    for h in range(heads):
        solved = dot_nn(
            jnp.concatenate([turned_units[h], rights[h]], axis=0), inverse[h].astype(BF16)
        ).astype(BF16)
        bt_ref[:, columns(h)] = solved[:length]
        cct_ref[:, columns(h)] = solved[length:]
        moved = dot_nn(solved, units[h])
        d_ref[:, columns(h)] = moved[:length].astype(BF16)
        c_ref[:, columns(h)] = (k_ref[:, columns(h)].astype(F32) - moved[length:]).astype(BF16)
    copies[3].wait()


def pair_kernel(c_ref, d_ref, other_ref, _, x2_ref, e_ref):
    length = c_ref.shape[0]
    for h in range(c_ref.shape[1] // HEAD_DIM):
        c, d, o = c_ref[:, columns(h)], d_ref[:, columns(h)], other_ref[:, columns(h)]
        both = dot_nn(jnp.concatenate([c, d], axis=0), o)
        x2_ref[:, columns(h)] = (c.astype(F32) - both[:length]).astype(BF16)
        e_ref[:, columns(h)] = (d.astype(F32) + o.astype(F32) - both[length:]).astype(BF16)


def third_kernel(near_ref, e_ref, x3_ref):
    for h in range(e_ref.shape[1] // HEAD_DIM):
        x = near_ref[:, columns(h)]
        x3_ref[:, columns(h)] = (x.astype(F32) - dot_nn(x, e_ref[:, columns(h)])).astype(BF16)


def query_kernel(
    visits_hbm, seg_ref, q_ref, k_ref, wb_ref, bt_ref, cct_ref, other_ref,
    t_ref, t2_ref, own_ref, gate_ref, visits_ref, sem,
):
    copy = pltpu.make_async_copy(visits_hbm, visits_ref, sem)
    copy.start()
    length, width = q_ref.shape
    row = lax.broadcasted_iota(jnp.int32, (length, length), 0)
    col = lax.broadcasted_iota(jnp.int32, (length, length), 1)
    block = lax.axis_index("seq")
    odd = lax.rem(block, 2)
    for group in range(0, width // HEAD_DIM, GROUP):
        cs = [columns(h) for h in range(group, group + GROUP)]
        both = [
            dot_nt(q_ref[:, c], jnp.concatenate([wb_ref[:, c], k_ref[:, c]], axis=0)) for c in cs
        ]
        query_w = [jnp.where(col <= row, b[:, :length], 0.0) for b in both]
        high = [w.astype(BF16) for w in query_w]
        low = [(w - h.astype(F32)).astype(BF16) for w, h in zip(query_w, high)]
        turn = [
            dot_nt(
                jnp.concatenate([h, w], axis=0),
                jnp.concatenate([bt_ref[:, c], cct_ref[:, c]], axis=0),
            )
            for h, w, c in zip(high, low, cs)
        ]
        turn = [t[:length] + t[length:] for t in turn]
        exact = [(q_ref[:, c].astype(F32) - t[:, :length]) * SCALE for t, c in zip(turn, cs)]
        rounded = [t.astype(BF16) for t in exact]
        shift = [dot_nt(t, other_ref[:, c]) for t, c in zip(rounded, cs)]
        for b, t, e, r, x, c in zip(both, turn, exact, rounded, shift, cs):
            own_ref[:, c] = (b[:, length:] - t[:, length:]) * SCALE
            t_ref[:, c] = r
            t2_ref[:, c] = (e - jnp.where(odd == 1, x, 0.0)).astype(BF16)

    def seg_row(back):
        return seg_ref[pl.ds(jnp.maximum(block - back, 0), 1), :].astype(F32)

    seg_q = jnp.transpose(jnp.broadcast_to(seg_row(0), (length, length)))
    copy.wait()
    for back in range(BACK + 1):
        allowed = seg_q == seg_row(back)
        if back == 0:
            allowed = allowed & (col <= row)
        else:
            allowed = allowed & (jnp.where(block - back >= 0, visits_ref[0, back - 1], 0) > 0)
        gate_ref[back] = jnp.where(allowed, 0.0, -1e30)


def near_kernel(gate_ref, t_ref, own_ref, near_ref, _, __, score_ref):
    for h in range(t_ref.shape[1] // HEAD_DIM):
        c = columns(h)
        score_ref[0, :, c] = own_ref[:, c] + gate_ref[0]
        score_ref[1, :, c] = dot_nt(t_ref[:, c], near_ref[:, c]) + gate_ref[1]


def by_parity(even, odd):
    parity = lax.rem(lax.axis_index("seq"), 2)
    pl.when(parity == 0)(even)
    pl.when(parity == 1)(odd)


def mid_kernel(
    gate_ref, t2_ref, score_ref, v_ref, early_ref, swapped_ref, pair_v_ref, even2, odd2,
    acc_ref, top_ref, total_ref,
):
    def run(far, v1):
        for group in range(0, t2_ref.shape[1] // HEAD_DIM, GROUP):
            cs = [columns(h) for h in range(group, group + GROUP)]
            score = [dot_nt(t2_ref[:, c], far[:, c]) + gate_ref[2] for c in cs]
            score = [
                jnp.concatenate([x, score_ref[1, :, c], score_ref[0, :, c]], axis=1)
                for x, c in zip(score, cs)
            ]
            top = [jnp.max(x, axis=-1, keepdims=True) for x in score]
            weights = [jnp.exp2(x - m) for x, m in zip(score, top)]
            for x, m, c in zip(weights, top, cs):
                rows = [early_ref[:, c], v1[:, c], v_ref[:, c]]
                acc_ref[:, c] = dot_nn(x.astype(BF16), jnp.concatenate(rows, axis=0))
                total = jnp.sum(x, axis=-1, keepdims=True)
                top_ref[:, c] = jnp.broadcast_to(m, acc_ref[:, c].shape)
                total_ref[:, c] = jnp.broadcast_to(total, acc_ref[:, c].shape)

    by_parity(lambda: run(even2, swapped_ref), lambda: run(odd2, pair_v_ref))


def final_kernel(
    gate_ref, t2_ref, acc_ref, top_ref, total_ref, even3, direct, odd3, swapped,
    out_hbm, out_ref, sems,
):
    heads = t2_ref.shape[1] // HEAD_DIM

    def copy(group):
        part = slice(group * HEAD_DIM, (group + GROUP) * HEAD_DIM)
        return pltpu.make_async_copy(out_ref.at[:, part], out_hbm.at[:, part], sems.at[group])

    def run(far, v3):
        for group in range(0, heads, GROUP):
            cs = [columns(h) for h in range(group, group + GROUP)]
            score = [dot_nt(t2_ref[:, c], far[:, c]) + gate_ref[3] for c in cs]
            top = [
                jnp.maximum(jnp.max(x, axis=-1, keepdims=True), top_ref[:, c])
                for x, c in zip(score, cs)
            ]
            weights = [jnp.exp2(x - m) for x, m in zip(score, top)]
            shrink = [jnp.exp2(top_ref[:, c] - m) for m, c in zip(top, cs)]
            mixed = [dot_nn(x.astype(BF16), v3[:, c]) for x, c in zip(weights, cs)]
            for x, m, p, c in zip(weights, mixed, shrink, cs):
                total = jnp.sum(x, axis=-1, keepdims=True) + p * total_ref[:, c]
                out_ref[:, c] = ((m + p * acc_ref[:, c]) / total).astype(BF16)
            copy(group).start()

    by_parity(lambda: run(even3, direct), lambda: run(odd3, swapped))
    for group in range(0, heads, GROUP):
        copy(group).wait()


def call(body, outs, *args, scratch=(), specs=None, out_specs=None, name=None):
    kept = pl.BlockSpec(memory_space=pltpu.VMEM)
    return pl.pallas_call(
        body,
        out_shape=outs,
        in_specs=specs or [kept] * len(args),
        out_specs=out_specs or [kept] * len(outs),
        scratch_shapes=scratch,
        compiler_params=pltpu.CompilerParams(vmem_limit_bytes=32 << 20),
        cost_estimate=pl.CostEstimate(flops=0, bytes_accessed=0, transcendentals=0),
        name=name,
    )(*args)


def shards(queries, keys, values, transitions, betas, segments, visits):
    shape = jax.ShapeDtypeStruct(queries.shape, BF16)
    wide = jax.ShapeDtypeStruct(queries.shape, F32)
    two_wide = jax.ShapeDtypeStruct((2, *queries.shape), F32)
    gates = jax.ShapeDtypeStruct((BACK + 1, queries.shape[0], queries.shape[0]), F32)
    size = lax.axis_size("seq")
    next_one = [(i, i + 1) for i in range(size - 1)]
    odd_three = [(i, i + 3) for i in range(1, size - 3, 2)]
    swap = [(i, i ^ 1) for i in range(size)]
    next_two = [(i, i + 2) for i in range(size - 2)]
    next_even = [(i, i + 2) for i in range(0, size - 2, 2)]
    to_odd = [(i, i + 1) for i in range(0, size, 2)]
    vmem = pl.BlockSpec(memory_space=pltpu.VMEM)
    smem = pl.BlockSpec(memory_space=pltpu.SMEM)
    hbm = pl.BlockSpec(memory_space=pltpu.HBM)
    anywhere = pl.BlockSpec(memory_space=pl.ANY)
    buffer = pltpu.VMEM(queries.shape, BF16)

    def sems(count):
        return pltpu.SemaphoreType.DMA((count,))

    unit, back_t, coef_t, carried, op, keys_, queries_ = call(
        prep_kernel,
        [shape] * 7,
        pltpu.with_memory_space_constraint(keys, pltpu.HBM),
        pltpu.with_memory_space_constraint(transitions, pltpu.HBM),
        pltpu.with_memory_space_constraint(betas.T, pltpu.HBM),
        pltpu.with_memory_space_constraint(queries, pltpu.HBM),
        specs=[hbm] * 4,
        scratch=[buffer, pltpu.VMEM(betas.shape[::-1], BF16), sems(4)],
        name="prep",
    )
    near_k = lax.ppermute(carried, "seq", next_one)
    other = lax.ppermute(op, "seq", swap)
    later, _ = lax.optimization_barrier((values, carried))
    direct = lax.ppermute(later, "seq", odd_three)
    turned, turned2, own, gate = call(
        query_kernel,
        [shape, shape, wide, gates],
        pltpu.with_memory_space_constraint(visits, pltpu.HBM),
        segments.reshape(size, -1),
        queries_,
        keys_,
        unit,
        back_t,
        coef_t,
        other,
        specs=[hbm] + [vmem] * 7,
        scratch=[pltpu.SMEM(visits.shape, jnp.int32), pltpu.SemaphoreType.DMA],
        name="query",
    )
    later, _ = lax.optimization_barrier((values, turned))
    early = lax.ppermute(later, "seq", next_two)
    second, both = call(
        pair_kernel,
        [shape, shape],
        carried,
        op,
        other,
        turned,
        specs=[vmem] * 3 + [anywhere],
        name="pair",
    )
    even2 = lax.ppermute(second, "seq", next_even)
    (third,) = call(
        third_kernel,
        [shape],
        near_k,
        both,
        name="third",
    )
    even3 = lax.ppermute(third, "seq", next_even)
    (scores,) = call(
        near_kernel,
        [two_wide],
        gate,
        turned,
        own,
        near_k,
        third,
        direct,
        specs=[vmem] * 4 + [anywhere] * 2,
        name="near",
    )
    near_k_, early_, values_, _ = lax.optimization_barrier((near_k, early, values, third))
    odd2 = lax.ppermute(near_k_, "seq", to_odd)
    swapped = lax.ppermute(early_, "seq", swap)
    pair_v = lax.ppermute(values_, "seq", swap)
    even2_, scores = lax.optimization_barrier((even2, scores))
    odd3 = lax.ppermute(even2_, "seq", to_odd)
    acc, top, total = call(
        mid_kernel,
        [wide, wide, wide],
        gate,
        turned2,
        scores,
        values,
        early,
        swapped,
        pair_v,
        even2,
        odd2,
        name="mid",
    )
    (out,) = call(
        final_kernel,
        [shape],
        gate,
        turned2,
        acc,
        top,
        total,
        even3,
        direct,
        odd3,
        swapped,
        out_specs=[hbm],
        scratch=[buffer, sems(queries.shape[1] // HEAD_DIM)],
        name="final",
    )
    return out


def solution(mesh):
    return jax.shard_map(
        shards,
        mesh=mesh,
        in_specs=(
            P("seq", "head"),
            P("seq", "head"),
            P("seq", "head"),
            P("seq", "head"),
            P("seq", "head"),
            P(),
            P("seq", None),
        ),
        out_specs=P("seq", "head"),
        check_vma=False,
    )
```

```python
import math

import jax
import jax.numpy as jnp
from jax import lax
from jax.experimental import pallas as pl
from jax.experimental.pallas import tpu as pltpu
from jax.sharding import PartitionSpec as P

HEAD_DIM = 128
BACK = 3
EPSILON = 1e-06
GROUP = 4
F32 = jnp.float32
BF16 = jnp.bfloat16
SCALE = HEAD_DIM**-0.5 * math.log2(math.e)


def dot_nn(left, right):
    return lax.dot_general(left, right, (((1,), (0,)), ((), ())), preferred_element_type=F32)


def dot_nt(left, right):
    return lax.dot_general(left, right, (((1,), (1,)), ((), ())), preferred_element_type=F32)


def columns(head):
    return slice(head * HEAD_DIM, (head + 1) * HEAD_DIM)


def pairs(width):
    return [slice(at, at + 2 * HEAD_DIM) for at in range(0, width, 2 * HEAD_DIM)]


def blocks(two):
    zero = jnp.zeros((two.shape[0], HEAD_DIM), two.dtype)
    return jnp.concatenate(
        [
            jnp.concatenate([two[:, :HEAD_DIM], zero], axis=1),
            jnp.concatenate([zero, two[:, HEAD_DIM:]], axis=1),
        ],
        axis=0,
    )


def upper_inverse(strict_uppers, row, col):
    size = row.shape[0]
    eye = jnp.where(row == col, 1.0, 0.0).astype(F32)
    base = 16
    same = (row // base) == (col // base)
    diag = [jnp.where(same, u, 0.0) for u in strict_uppers]
    first = [d.astype(BF16) for d in diag]
    power = [dot_nn(p, blocks(p)).astype(BF16) for p in first]
    inverse = [eye - d for d in diag]
    reach = 4
    while reach < base:
        both = [
            dot_nn(jnp.concatenate([x.astype(BF16), p], axis=0), blocks(p))
            for x, p in zip(inverse, power)
        ]
        inverse = [x + b[:size] for x, b in zip(inverse, both)]
        power = [b[size:].astype(BF16) for b in both]
        reach *= 2
    inverse = [x + dot_nn(x.astype(BF16), blocks(p)) for x, p in zip(inverse, power)]
    span = 2 * base
    while span <= size:
        joined = ((row // span) == (col // span)) & ((row // (span // 2)) != (col // (span // 2)))
        corner = [jnp.where(joined, u, 0.0).astype(BF16) for u in strict_uppers]
        half = [x.astype(BF16) for x in inverse]
        mid = [dot_nn(x, blocks(e)).astype(BF16) for x, e in zip(half, corner)]
        inverse = [x - dot_nn(m, blocks(y)) for x, m, y in zip(inverse, mid, half)]
        span *= 2
    return inverse


def prep_kernel(
    k_hbm, w_hbm, beta_hbm, q_hbm, wb_ref, bt_ref, cct_ref, c_ref, d_ref, k_ref, q_ref,
    w_ref, beta_ref, sems,
):
    length, width = k_ref.shape
    copies = [
        pltpu.make_async_copy(w_hbm, w_ref, sems.at[0]),
        pltpu.make_async_copy(beta_hbm, beta_ref, sems.at[2]),
        pltpu.make_async_copy(k_hbm, k_ref, sems.at[1]),
        pltpu.make_async_copy(q_hbm, q_ref, sems.at[3]),
    ]
    for copy in copies:
        copy.start()
    heads = width // HEAD_DIM
    row = lax.broadcasted_iota(jnp.int32, (length, 2 * length), 0)
    col = lax.rem(lax.broadcasted_iota(jnp.int32, (length, 2 * length), 1), length)
    upper = row < col
    copies[0].wait()
    copies[1].wait()
    beta = beta_ref[...].astype(F32)
    beta = jnp.transpose(jnp.concatenate([beta] * (length // heads), axis=0))
    scaled, turned_units = [], []
    for h in range(heads):
        w = w_ref[:, columns(h)].astype(F32)
        scale = lax.rsqrt(jnp.sum(w * w, axis=-1, keepdims=True) + EPSILON)
        unit = w * scale
        bw = unit * beta[:, h : h + 1]
        scaled.append(bw.astype(BF16))
        turned_units.append(jnp.transpose(bw).astype(BF16))
        wb_ref[:, columns(h)] = unit.astype(BF16)
    copies[2].wait()
    both = []
    for i, c in enumerate(pairs(width)):
        right = blocks(jnp.concatenate(scaled[2 * i : 2 * i + 2], axis=1))
        both.append(dot_nt(jnp.concatenate([wb_ref[:, c], k_ref[:, c]], axis=0), right))
    uppers = [jnp.where(upper, b[:length], 0.0) for b in both]
    rights = [jnp.where(upper, b[length:], 0.0).astype(BF16) for b in both]
    inverse = upper_inverse(uppers, row, col)
    solved = []
    for i, (r, x) in enumerate(zip(rights, inverse)):
        left = jnp.concatenate(turned_units[2 * i : 2 * i + 2], axis=1)
        left = jnp.concatenate([left, r], axis=0)
        solved.append(dot_nn(left, blocks(x.astype(BF16))).astype(BF16))
    for c, x in zip(pairs(width), solved):
        moved = dot_nn(x, blocks(wb_ref[:, c]))
        c_ref[:, c] = (k_ref[:, c].astype(F32) - moved[length:]).astype(BF16)
        d_ref[:, c] = moved[:length].astype(BF16)
        bt_ref[:, c] = x[:length]
        cct_ref[:, c] = x[length:]
    copies[3].wait()


def pair_kernel(c_ref, d_ref, other_ref, _, x2_ref, e_ref):
    length = c_ref.shape[0]
    for h in range(c_ref.shape[1] // HEAD_DIM):
        c, d, o = c_ref[:, columns(h)], d_ref[:, columns(h)], other_ref[:, columns(h)]
        both = dot_nn(jnp.concatenate([c, d], axis=0), o)
        x2_ref[:, columns(h)] = (c.astype(F32) - both[:length]).astype(BF16)
        e_ref[:, columns(h)] = (d.astype(F32) + o.astype(F32) - both[length:]).astype(BF16)


def third_kernel(near_ref, e_ref, x3_ref):
    for c in pairs(e_ref.shape[1]):
        x = near_ref[:, c]
        x3_ref[:, c] = (x.astype(F32) - dot_nn(x, blocks(e_ref[:, c]))).astype(BF16)


def query_kernel(
    visits_hbm, seg_ref, q_ref, k_ref, wb_ref, bt_ref, cct_ref, other_ref,
    t_ref, t2_ref, own_ref, gate_ref, visits_ref, sem,
):
    copy = pltpu.make_async_copy(visits_hbm, visits_ref, sem)
    copy.start()
    length, width = q_ref.shape
    row = lax.broadcasted_iota(jnp.int32, (length, length), 0)
    col = lax.broadcasted_iota(jnp.int32, (length, length), 1)
    block = lax.axis_index("seq")
    odd = lax.rem(block, 2)
    for group in range(0, width // HEAD_DIM, GROUP):
        cs = [columns(h) for h in range(group, group + GROUP)]
        both = [
            dot_nt(q_ref[:, c], jnp.concatenate([wb_ref[:, c], k_ref[:, c]], axis=0)) for c in cs
        ]
        query_w = [jnp.where(col <= row, b[:, :length], 0.0) for b in both]
        high = [w.astype(BF16) for w in query_w]
        low = [(w - h.astype(F32)).astype(BF16) for w, h in zip(query_w, high)]
        turn = [
            dot_nt(
                jnp.concatenate([h, w], axis=0),
                jnp.concatenate([bt_ref[:, c], cct_ref[:, c]], axis=0),
            )
            for h, w, c in zip(high, low, cs)
        ]
        turn = [t[:length] + t[length:] for t in turn]
        exact = [(q_ref[:, c].astype(F32) - t[:, :length]) * SCALE for t, c in zip(turn, cs)]
        rounded = [t.astype(BF16) for t in exact]
        shift = [dot_nt(t, other_ref[:, c]) for t, c in zip(rounded, cs)]
        for b, t, e, r, x, c in zip(both, turn, exact, rounded, shift, cs):
            own_ref[:, c] = (b[:, length:] - t[:, length:]) * SCALE
            t_ref[:, c] = r
            t2_ref[:, c] = (e - jnp.where(odd == 1, x, 0.0)).astype(BF16)

    def seg_row(back):
        return seg_ref[pl.ds(jnp.maximum(block - back, 0), 1), :].astype(F32)

    seg_q = jnp.transpose(jnp.broadcast_to(seg_row(0), (length, length)))
    copy.wait()
    for back in range(BACK + 1):
        allowed = seg_q == seg_row(back)
        if back == 0:
            allowed = allowed & (col <= row)
        else:
            allowed = allowed & (jnp.where(block - back >= 0, visits_ref[0, back - 1], 0) > 0)
        gate_ref[back] = jnp.where(allowed, 0.0, -1e30)


def near_kernel(gate_ref, t_ref, own_ref, near_ref, _, __, score_ref):
    for h in range(t_ref.shape[1] // HEAD_DIM):
        c = columns(h)
        score_ref[0, :, c] = own_ref[:, c] + gate_ref[0]
        score_ref[1, :, c] = dot_nt(t_ref[:, c], near_ref[:, c]) + gate_ref[1]


def by_parity(even, odd):
    parity = lax.rem(lax.axis_index("seq"), 2)
    pl.when(parity == 0)(even)
    pl.when(parity == 1)(odd)


def mid_kernel(
    gate_ref, t2_ref, score_ref, v_ref, early_ref, swapped_ref, pair_v_ref, even2, odd2,
    acc_ref, top_ref, total_ref,
):
    def run(far, v1):
        for group in range(0, t2_ref.shape[1] // HEAD_DIM, GROUP):
            cs = [columns(h) for h in range(group, group + GROUP)]
            score = [dot_nt(t2_ref[:, c], far[:, c]) + gate_ref[2] for c in cs]
            score = [
                jnp.concatenate([x, score_ref[1, :, c], score_ref[0, :, c]], axis=1)
                for x, c in zip(score, cs)
            ]
            top = [jnp.max(x, axis=-1, keepdims=True) for x in score]
            weights = [jnp.exp2(x - m) for x, m in zip(score, top)]
            for x, m, c in zip(weights, top, cs):
                rows = [early_ref[:, c], v1[:, c], v_ref[:, c]]
                acc_ref[:, c] = dot_nn(x.astype(BF16), jnp.concatenate(rows, axis=0))
                total = jnp.sum(x, axis=-1, keepdims=True)
                top_ref[:, c] = jnp.broadcast_to(m, acc_ref[:, c].shape)
                total_ref[:, c] = jnp.broadcast_to(total, acc_ref[:, c].shape)

    by_parity(lambda: run(even2, swapped_ref), lambda: run(odd2, pair_v_ref))


def final_kernel(
    gate_ref, t2_ref, acc_ref, top_ref, total_ref, even3, direct, odd3, swapped,
    out_hbm, out_ref, sems,
):
    heads = t2_ref.shape[1] // HEAD_DIM

    def copy(group):
        part = slice(group * HEAD_DIM, (group + GROUP) * HEAD_DIM)
        return pltpu.make_async_copy(out_ref.at[:, part], out_hbm.at[:, part], sems.at[group])

    def run(far, v3):
        for group in range(0, heads, GROUP):
            cs = [columns(h) for h in range(group, group + GROUP)]
            score = [dot_nt(t2_ref[:, c], far[:, c]) + gate_ref[3] for c in cs]
            top = [
                jnp.maximum(jnp.max(x, axis=-1, keepdims=True), top_ref[:, c])
                for x, c in zip(score, cs)
            ]
            weights = [jnp.exp2(x - m) for x, m in zip(score, top)]
            shrink = [jnp.exp2(top_ref[:, c] - m) for m, c in zip(top, cs)]
            mixed = [dot_nn(x.astype(BF16), v3[:, c]) for x, c in zip(weights, cs)]
            for x, m, p, c in zip(weights, mixed, shrink, cs):
                total = jnp.sum(x, axis=-1, keepdims=True) + p * total_ref[:, c]
                out_ref[:, c] = ((m + p * acc_ref[:, c]) / total).astype(BF16)
            copy(group).start()

    by_parity(lambda: run(even3, direct), lambda: run(odd3, swapped))
    for group in range(0, heads, GROUP):
        copy(group).wait()


def call(body, outs, *args, scratch=(), specs=None, out_specs=None, name=None):
    kept = pl.BlockSpec(memory_space=pltpu.VMEM)
    return pl.pallas_call(
        body,
        out_shape=outs,
        in_specs=specs or [kept] * len(args),
        out_specs=out_specs or [kept] * len(outs),
        scratch_shapes=scratch,
        compiler_params=pltpu.CompilerParams(vmem_limit_bytes=32 << 20),
        cost_estimate=pl.CostEstimate(flops=0, bytes_accessed=0, transcendentals=0),
        name=name,
    )(*args)


def shards(queries, keys, values, transitions, betas, segments, visits):
    shape = jax.ShapeDtypeStruct(queries.shape, BF16)
    wide = jax.ShapeDtypeStruct(queries.shape, F32)
    two_wide = jax.ShapeDtypeStruct((2, *queries.shape), F32)
    gates = jax.ShapeDtypeStruct((BACK + 1, queries.shape[0], queries.shape[0]), F32)
    size = lax.axis_size("seq")
    next_one = [(i, i + 1) for i in range(size - 1)]
    odd_three = [(i, i + 3) for i in range(1, size - 3, 2)]
    swap = [(i, i ^ 1) for i in range(size)]
    next_two = [(i, i + 2) for i in range(size - 2)]
    next_even = [(i, i + 2) for i in range(0, size - 2, 2)]
    to_odd = [(i, i + 1) for i in range(0, size, 2)]
    vmem = pl.BlockSpec(memory_space=pltpu.VMEM)
    smem = pl.BlockSpec(memory_space=pltpu.SMEM)
    hbm = pl.BlockSpec(memory_space=pltpu.HBM)
    anywhere = pl.BlockSpec(memory_space=pl.ANY)
    buffer = pltpu.VMEM(queries.shape, BF16)

    def sems(count):
        return pltpu.SemaphoreType.DMA((count,))

    unit, back_t, coef_t, carried, op, keys_, queries_ = call(
        prep_kernel,
        [shape] * 7,
        pltpu.with_memory_space_constraint(keys, pltpu.HBM),
        pltpu.with_memory_space_constraint(transitions, pltpu.HBM),
        pltpu.with_memory_space_constraint(betas.T, pltpu.HBM),
        pltpu.with_memory_space_constraint(queries, pltpu.HBM),
        specs=[hbm] * 4,
        scratch=[buffer, pltpu.VMEM(betas.shape[::-1], BF16), sems(4)],
        name="prep",
    )
    near_k = lax.ppermute(carried, "seq", next_one)
    other = lax.ppermute(op, "seq", swap)
    later, _ = lax.optimization_barrier((values, carried))
    early = lax.ppermute(later, "seq", next_two)
    turned, turned2, own, gate = call(
        query_kernel,
        [shape, shape, wide, gates],
        pltpu.with_memory_space_constraint(visits, pltpu.HBM),
        segments.reshape(size, -1),
        queries_,
        keys_,
        unit,
        back_t,
        coef_t,
        other,
        specs=[hbm] + [vmem] * 7,
        scratch=[pltpu.SMEM(visits.shape, jnp.int32), pltpu.SemaphoreType.DMA],
        name="query",
    )
    later, _ = lax.optimization_barrier((values, turned))
    direct = lax.ppermute(later, "seq", odd_three)
    second, both = call(
        pair_kernel,
        [shape, shape],
        carried,
        op,
        other,
        turned,
        specs=[vmem] * 3 + [anywhere],
        name="pair",
    )
    even2 = lax.ppermute(second, "seq", next_even)
    (third,) = call(
        third_kernel,
        [shape],
        near_k,
        both,
        name="third",
    )
    even3 = lax.ppermute(third, "seq", next_even)
    (scores,) = call(
        near_kernel,
        [two_wide],
        gate,
        turned,
        own,
        near_k,
        third,
        direct,
        specs=[vmem] * 4 + [anywhere] * 2,
        name="near",
    )
    near_k_, early_, values_, _ = lax.optimization_barrier((near_k, early, values, third))
    odd2 = lax.ppermute(near_k_, "seq", to_odd)
    swapped = lax.ppermute(early_, "seq", swap)
    pair_v = lax.ppermute(values_, "seq", swap)
    even2_, scores = lax.optimization_barrier((even2, scores))
    odd3 = lax.ppermute(even2_, "seq", to_odd)
    acc, top, total = call(
        mid_kernel,
        [wide, wide, wide],
        gate,
        turned2,
        scores,
        values,
        early,
        swapped,
        pair_v,
        even2,
        odd2,
        name="mid",
    )
    (out,) = call(
        final_kernel,
        [shape],
        gate,
        turned2,
        acc,
        top,
        total,
        even3,
        direct,
        odd3,
        swapped,
        out_specs=[hbm],
        scratch=[buffer, sems(queries.shape[1] // HEAD_DIM)],
        name="final",
    )
    return out


def solution(mesh):
    return jax.shard_map(
        shards,
        mesh=mesh,
        in_specs=(
            P("seq", "head"),
            P("seq", "head"),
            P("seq", "head"),
            P("seq", "head"),
            P("seq", "head"),
            P(),
            P("seq", None),
        ),
        out_specs=P("seq", "head"),
        check_vma=False,
    )
```

```python
import math

import jax
import jax.numpy as jnp
from jax import lax
from jax.experimental import pallas as pl
from jax.experimental.pallas import tpu as pltpu
from jax.sharding import PartitionSpec as P

HEAD_DIM = 128
BACK = 3
EPSILON = 1e-06
GROUP = 4
LAST_GROUP = 4
F32 = jnp.float32
BF16 = jnp.bfloat16
SCALE = HEAD_DIM**-0.5 * math.log2(math.e)


def dot_nn(left, right):
    return lax.dot_general(left, right, (((1,), (0,)), ((), ())), preferred_element_type=F32)


def dot_nt(left, right):
    return lax.dot_general(left, right, (((1,), (1,)), ((), ())), preferred_element_type=F32)


def columns(head):
    return slice(head * HEAD_DIM, (head + 1) * HEAD_DIM)


def pairs(width):
    return [slice(at, at + 2 * HEAD_DIM) for at in range(0, width, 2 * HEAD_DIM)]


def blocks(two):
    zero = jnp.zeros((two.shape[0], HEAD_DIM), two.dtype)
    return jnp.concatenate(
        [
            jnp.concatenate([two[:, :HEAD_DIM], zero], axis=1),
            jnp.concatenate([zero, two[:, HEAD_DIM:]], axis=1),
        ],
        axis=0,
    )


def upper_inverse(strict_uppers, row, col):
    size = row.shape[0]
    eye = jnp.where(row == col, 1.0, 0.0).astype(F32)
    base = 16
    same = (row // base) == (col // base)
    diag = [jnp.where(same, u, 0.0) for u in strict_uppers]
    first = [d.astype(BF16) for d in diag]
    power = [dot_nn(p, blocks(p)).astype(BF16) for p in first]
    inverse = [eye - d for d in diag]
    reach = 4
    while reach < base:
        both = [
            dot_nn(jnp.concatenate([x.astype(BF16), p], axis=0), blocks(p))
            for x, p in zip(inverse, power)
        ]
        inverse = [x + b[:size] for x, b in zip(inverse, both)]
        power = [b[size:].astype(BF16) for b in both]
        reach *= 2
    inverse = [x + dot_nn(x.astype(BF16), blocks(p)) for x, p in zip(inverse, power)]
    span = 2 * base
    while span <= size:
        joined = ((row // span) == (col // span)) & ((row // (span // 2)) != (col // (span // 2)))
        corner = [jnp.where(joined, u, 0.0).astype(BF16) for u in strict_uppers]
        half = [x.astype(BF16) for x in inverse]
        mid = [dot_nn(x, blocks(e)).astype(BF16) for x, e in zip(half, corner)]
        inverse = [x - dot_nn(m, blocks(y)) for x, m, y in zip(inverse, mid, half)]
        span *= 2
    return inverse


def prep_kernel(
    k_hbm, w_hbm, beta_hbm, q_hbm, wb_ref, bt_ref, cct_ref, c_ref, d_ref, k_ref, q_ref,
    w_ref, beta_ref, sems,
):
    length, width = k_ref.shape
    copies = [
        pltpu.make_async_copy(w_hbm, w_ref, sems.at[0]),
        pltpu.make_async_copy(beta_hbm, beta_ref, sems.at[2]),
        pltpu.make_async_copy(k_hbm, k_ref, sems.at[1]),
        pltpu.make_async_copy(q_hbm, q_ref, sems.at[3]),
    ]
    for copy in copies:
        copy.start()
    heads = width // HEAD_DIM
    row = lax.broadcasted_iota(jnp.int32, (length, 2 * length), 0)
    col = lax.rem(lax.broadcasted_iota(jnp.int32, (length, 2 * length), 1), length)
    upper = row < col
    copies[0].wait()
    copies[1].wait()
    beta = beta_ref[...].astype(F32)
    beta = jnp.transpose(jnp.concatenate([beta] * (length // heads), axis=0))
    scaled, turned_units = [], []
    for h in range(heads):
        w = w_ref[:, columns(h)].astype(F32)
        scale = lax.rsqrt(jnp.sum(w * w, axis=-1, keepdims=True) + EPSILON)
        unit = w * scale
        bw = unit * beta[:, h : h + 1]
        scaled.append(bw.astype(BF16))
        turned_units.append(jnp.transpose(bw).astype(BF16))
        wb_ref[:, columns(h)] = unit.astype(BF16)
    copies[2].wait()
    both = []
    for i, c in enumerate(pairs(width)):
        right = blocks(jnp.concatenate(scaled[2 * i : 2 * i + 2], axis=1))
        both.append(dot_nt(jnp.concatenate([wb_ref[:, c], k_ref[:, c]], axis=0), right))
    uppers = [jnp.where(upper, b[:length], 0.0) for b in both]
    rights = [jnp.where(upper, b[length:], 0.0).astype(BF16) for b in both]
    inverse = upper_inverse(uppers, row, col)
    solved = []
    for i, (r, x) in enumerate(zip(rights, inverse)):
        left = jnp.concatenate(turned_units[2 * i : 2 * i + 2], axis=1)
        left = jnp.concatenate([left, r], axis=0)
        solved.append(dot_nn(left, blocks(x.astype(BF16))).astype(BF16))
    for c, x in zip(pairs(width), solved):
        moved = dot_nn(x, blocks(wb_ref[:, c]))
        c_ref[:, c] = (k_ref[:, c].astype(F32) - moved[length:]).astype(BF16)
        d_ref[:, c] = moved[:length].astype(BF16)
        bt_ref[:, c] = x[:length]
        cct_ref[:, c] = x[length:]
    copies[3].wait()


def pair_kernel(c_ref, d_ref, other_ref, _, x2_ref, e_ref):
    length = c_ref.shape[0]
    for h in range(c_ref.shape[1] // HEAD_DIM):
        c, d, o = c_ref[:, columns(h)], d_ref[:, columns(h)], other_ref[:, columns(h)]
        both = dot_nn(jnp.concatenate([c, d], axis=0), o)
        x2_ref[:, columns(h)] = (c.astype(F32) - both[:length]).astype(BF16)
        e_ref[:, columns(h)] = (d.astype(F32) + o.astype(F32) - both[length:]).astype(BF16)


def third_kernel(near_ref, e_ref, x3_ref):
    for c in pairs(e_ref.shape[1]):
        x = near_ref[:, c]
        x3_ref[:, c] = (x.astype(F32) - dot_nn(x, blocks(e_ref[:, c]))).astype(BF16)


def query_kernel(
    visits_hbm, seg_ref, q_ref, k_ref, wb_ref, bt_ref, cct_ref, other_ref,
    t_ref, t2_ref, own_ref, gate_ref, visits_ref, sem,
):
    copy = pltpu.make_async_copy(visits_hbm, visits_ref, sem)
    copy.start()
    length, width = q_ref.shape
    row = lax.broadcasted_iota(jnp.int32, (length, length), 0)
    col = lax.broadcasted_iota(jnp.int32, (length, length), 1)
    block = lax.axis_index("seq")
    odd = lax.rem(block, 2)
    for group in range(0, width // HEAD_DIM, GROUP):
        cs = [columns(h) for h in range(group, group + GROUP)]
        both = [
            dot_nt(q_ref[:, c], jnp.concatenate([wb_ref[:, c], k_ref[:, c]], axis=0)) for c in cs
        ]
        query_w = [jnp.where(col <= row, b[:, :length], 0.0) for b in both]
        high = [w.astype(BF16) for w in query_w]
        low = [(w - h.astype(F32)).astype(BF16) for w, h in zip(query_w, high)]
        turn = [
            dot_nt(
                jnp.concatenate([h, w], axis=0),
                jnp.concatenate([bt_ref[:, c], cct_ref[:, c]], axis=0),
            )
            for h, w, c in zip(high, low, cs)
        ]
        turn = [t[:length] + t[length:] for t in turn]
        exact = [(q_ref[:, c].astype(F32) - t[:, :length]) * SCALE for t, c in zip(turn, cs)]
        rounded = [t.astype(BF16) for t in exact]
        shift = [dot_nt(t, other_ref[:, c]) for t, c in zip(rounded, cs)]
        for b, t, e, r, x, c in zip(both, turn, exact, rounded, shift, cs):
            own_ref[:, c] = (b[:, length:] - t[:, length:]) * SCALE
            t_ref[:, c] = r
            t2_ref[:, c] = (e - jnp.where(odd == 1, x, 0.0)).astype(BF16)

    def seg_row(back):
        return seg_ref[pl.ds(jnp.maximum(block - back, 0), 1), :].astype(F32)

    seg_q = jnp.transpose(jnp.broadcast_to(seg_row(0), (length, length)))
    copy.wait()
    for back in range(BACK + 1):
        allowed = seg_q == seg_row(back)
        if back == 0:
            allowed = allowed & (col <= row)
        else:
            allowed = allowed & (jnp.where(block - back >= 0, visits_ref[0, back - 1], 0) > 0)
        gate_ref[back] = jnp.where(allowed, 0.0, -1e30)


def near_kernel(gate_ref, t_ref, own_ref, near_ref, _, score_ref):
    for h in range(t_ref.shape[1] // HEAD_DIM):
        c = columns(h)
        score_ref[0, :, c] = own_ref[:, c] + gate_ref[0]
        score_ref[1, :, c] = dot_nt(t_ref[:, c], near_ref[:, c]) + gate_ref[1]


def by_parity(even, odd):
    parity = lax.rem(lax.axis_index("seq"), 2)
    pl.when(parity == 0)(even)
    pl.when(parity == 1)(odd)


def mid_kernel(
    gate_ref, t2_ref, score_ref, v_ref, early_ref, swapped_ref, pair_v_ref, even2, odd2,
    acc_ref, top_ref, total_ref,
):
    def run(far, v1):
        for group in range(0, t2_ref.shape[1] // HEAD_DIM, GROUP):
            cs = [columns(h) for h in range(group, group + GROUP)]
            score = [dot_nt(t2_ref[:, c], far[:, c]) + gate_ref[2] for c in cs]
            score = [
                jnp.concatenate([x, score_ref[1, :, c], score_ref[0, :, c]], axis=1)
                for x, c in zip(score, cs)
            ]
            top = [jnp.max(x, axis=-1, keepdims=True) for x in score]
            weights = [jnp.exp2(x - m) for x, m in zip(score, top)]
            for x, m, c in zip(weights, top, cs):
                rows = [early_ref[:, c], v1[:, c], v_ref[:, c]]
                acc_ref[:, c] = dot_nn(x.astype(BF16), jnp.concatenate(rows, axis=0))
                total = jnp.sum(x, axis=-1, keepdims=True)
                top_ref[:, c] = jnp.broadcast_to(m, acc_ref[:, c].shape)
                total_ref[:, c] = jnp.broadcast_to(total, acc_ref[:, c].shape)

    by_parity(lambda: run(even2, swapped_ref), lambda: run(odd2, pair_v_ref))


def final_kernel(
    gate_ref, t2_ref, acc_ref, top_ref, total_ref, even3, direct, odd3, swapped,
    out_hbm, out_ref, sems,
):
    heads = t2_ref.shape[1] // HEAD_DIM

    def copy(group):
        part = slice(group * HEAD_DIM, (group + LAST_GROUP) * HEAD_DIM)
        return pltpu.make_async_copy(out_ref.at[:, part], out_hbm.at[:, part], sems.at[group])

    def run(far, v3):
        for group in range(0, heads, LAST_GROUP):
            cs = [columns(h) for h in range(group, group + LAST_GROUP)]
            score = [dot_nt(t2_ref[:, c], far[:, c]) + gate_ref[3] for c in cs]
            top = [
                jnp.maximum(jnp.max(x, axis=-1, keepdims=True), top_ref[:, c])
                for x, c in zip(score, cs)
            ]
            weights = [jnp.exp2(x - m) for x, m in zip(score, top)]
            shrink = [jnp.exp2(top_ref[:, c] - m) for m, c in zip(top, cs)]
            mixed = [dot_nn(x.astype(BF16), v3[:, c]) for x, c in zip(weights, cs)]
            for x, m, p, c in zip(weights, mixed, shrink, cs):
                total = jnp.sum(x, axis=-1, keepdims=True) + p * total_ref[:, c]
                out_ref[:, c] = ((m + p * acc_ref[:, c]) / total).astype(BF16)
            copy(group).start()

    by_parity(lambda: run(even3, direct), lambda: run(odd3, swapped))
    for group in range(0, heads, LAST_GROUP):
        copy(group).wait()


def call(body, outs, *args, scratch=(), specs=None, out_specs=None, name=None):
    kept = pl.BlockSpec(memory_space=pltpu.VMEM)
    return pl.pallas_call(
        body,
        out_shape=outs,
        in_specs=specs or [kept] * len(args),
        out_specs=out_specs or [kept] * len(outs),
        scratch_shapes=scratch,
        compiler_params=pltpu.CompilerParams(vmem_limit_bytes=32 << 20),
        cost_estimate=pl.CostEstimate(flops=0, bytes_accessed=0, transcendentals=0),
        name=name,
    )(*args)


def shards(queries, keys, values, transitions, betas, segments, visits):
    shape = jax.ShapeDtypeStruct(queries.shape, BF16)
    wide = jax.ShapeDtypeStruct(queries.shape, F32)
    two_wide = jax.ShapeDtypeStruct((2, *queries.shape), F32)
    gates = jax.ShapeDtypeStruct((BACK + 1, queries.shape[0], queries.shape[0]), F32)
    size = lax.axis_size("seq")
    next_one = [(i, i + 1) for i in range(size - 1)]
    odd_three = [(i, i + 3) for i in range(1, size - 3, 2)]
    swap = [(i, i ^ 1) for i in range(size)]
    next_two = [(i, i + 2) for i in range(size - 2)]
    next_even = [(i, i + 2) for i in range(0, size - 2, 2)]
    to_odd = [(i, i + 1) for i in range(0, size, 2)]
    vmem = pl.BlockSpec(memory_space=pltpu.VMEM)
    smem = pl.BlockSpec(memory_space=pltpu.SMEM)
    hbm = pl.BlockSpec(memory_space=pltpu.HBM)
    anywhere = pl.BlockSpec(memory_space=pl.ANY)
    buffer = pltpu.VMEM(queries.shape, BF16)

    def sems(count):
        return pltpu.SemaphoreType.DMA((count,))

    unit, back_t, coef_t, carried, op, keys_, queries_ = call(
        prep_kernel,
        [shape] * 7,
        pltpu.with_memory_space_constraint(keys, pltpu.HBM),
        pltpu.with_memory_space_constraint(transitions, pltpu.HBM),
        pltpu.with_memory_space_constraint(betas.T, pltpu.HBM),
        pltpu.with_memory_space_constraint(queries, pltpu.HBM),
        specs=[hbm] * 4,
        scratch=[buffer, pltpu.VMEM(betas.shape[::-1], BF16), sems(4)],
        name="prep",
    )
    near_k = lax.ppermute(carried, "seq", next_one)
    other = lax.ppermute(op, "seq", swap)
    later, _ = lax.optimization_barrier((values, carried))
    early = lax.ppermute(later, "seq", next_two)
    turned, turned2, own, gate = call(
        query_kernel,
        [shape, shape, wide, gates],
        pltpu.with_memory_space_constraint(visits, pltpu.HBM),
        segments.reshape(size, -1),
        queries_,
        keys_,
        unit,
        back_t,
        coef_t,
        other,
        specs=[hbm] + [vmem] * 7,
        scratch=[pltpu.SMEM(visits.shape, jnp.int32), pltpu.SemaphoreType.DMA],
        name="query",
    )
    later, _ = lax.optimization_barrier((values, turned))
    direct = lax.ppermute(later, "seq", odd_three)
    second, both = call(
        pair_kernel,
        [shape, shape],
        carried,
        op,
        other,
        turned,
        specs=[vmem] * 3 + [anywhere],
        name="pair",
    )
    even2 = lax.ppermute(second, "seq", next_even)
    (third,) = call(
        third_kernel,
        [shape],
        near_k,
        both,
        name="third",
    )
    even3 = lax.ppermute(third, "seq", next_even)
    (scores,) = call(
        near_kernel,
        [two_wide],
        gate,
        turned,
        own,
        near_k,
        third,
        specs=[vmem] * 4 + [anywhere],
        name="near",
    )
    near_k_, early_, values_, _ = lax.optimization_barrier((near_k, early, values, third))
    odd2 = lax.ppermute(near_k_, "seq", to_odd)
    swapped = lax.ppermute(early_, "seq", swap)
    values_, direct, scores = lax.optimization_barrier((values_, direct, scores))
    pair_v = lax.ppermute(values_, "seq", swap)
    even2_, scores = lax.optimization_barrier((even2, scores))
    odd3 = lax.ppermute(even2_, "seq", to_odd)
    acc, top, total = call(
        mid_kernel,
        [wide, wide, wide],
        gate,
        turned2,
        scores,
        values,
        early,
        swapped,
        pair_v,
        even2,
        odd2,
        name="mid",
    )
    (out,) = call(
        final_kernel,
        [shape],
        gate,
        turned2,
        acc,
        top,
        total,
        even3,
        direct,
        odd3,
        swapped,
        out_specs=[hbm],
        scratch=[buffer, sems(queries.shape[1] // HEAD_DIM)],
        name="final",
    )
    return out


def solution(mesh):
    return jax.shard_map(
        shards,
        mesh=mesh,
        in_specs=(
            P("seq", "head"),
            P("seq", "head"),
            P("seq", "head"),
            P("seq", "head"),
            P("seq", "head"),
            P(),
            P("seq", None),
        ),
        out_specs=P("seq", "head"),
        check_vma=False,
    )
```
